32 devices in a mesh: gx: 4 (over y, x), yz: 8 (over z, core).
Axes of the slice: x: 2, y: 2, z: 4, core: 2. Of those that a mesh axis runs over, the one named last changes fastest.
Arguments:
- potential: float32 [32, 64, 2048], P('gx', 'yz'), may hold values from -96 to 96
- gal_cells: int32 [4, 8, 8, 128], P('gx', 'yz'), may hold values from 0 to 63
- gal_z: int32 [4, 8, 8, 128], P('gx', 'yz'), may hold values from 0 to 2047
- gal_bins: int32 [4, 8, 8, 128], P('gx', 'yz'), may hold values from 0 to 7
- gal_counts: int32 [4, 8, 8], P('gx', 'yz'), may hold values from 1 to 128, as said below
Outputs:
- tidal: float32 [6, 4, 8, 1024], P(None, 'gx', 'yz')
The draws below stay inside these ranges and needn't reach their ends.
Inputs may be any that keep to these rules, and one draw needn't show every extreme that they name: For each band g, one tile d receives 128 live slots from every home device; the live slots are the first gal_counts ones.
All inputs are finite; a program needn't handle non-finite values.
Results may differ from the reference program's by a relative error of at most 0.00002.
Values sent between devices are 32-bit elements; how exact they have to be, the bound alone decides.
No kernel may reach another device: no remote copies, remote signals or barrier semaphores. Data moves between devices by JAX's collectives and lax.ppermute only.
A program may use at most 192 MiB of HBM per device.

```python
import jax
import jax.numpy as jnp
from jax import lax

CX = 8
CY = 8
CZ = 2048
CAP = 128
HALO = 6
BINS = 8
NX = 32
NY = 64
N_GX = 4
N_YZ = 8


def draw_gal_counts(key, part):
    lowest = max(1, CAP // 4)
    counts = jax.random.randint(jax.random.fold_in(key, 11), (N_GX, N_YZ, N_YZ), lowest, CAP + 1)
    hot_tile = jax.random.randint(jax.random.fold_in(key, 12), (N_GX, 1, 1), 0, N_YZ)
    columns = lax.broadcasted_iota(jnp.int32, (N_GX, N_YZ, N_YZ), 2)
    return jnp.where(columns == hot_tile, CAP, counts).astype(jnp.int32)


def plant(drawn, key, least, high):
    shape = drawn.shape
    index_at = [jax.random.randint(jax.random.fold_in(key, axis), (), 0, shape[axis]) for axis in range(len(shape))]
    drawn = drawn.at[tuple(index_at)].set(least)
    longest = shape.index(max(shape))
    index_at[longest] = (index_at[longest] + 1) % shape[longest]
    return drawn.at[tuple(index_at)].set(high)


def steps_of(own_key, extent, split, smallest, top_value):
    gain = 1.0
    for axis_at, blocks in split:
        heights = jax.random.uniform(jax.random.fold_in(jax.random.fold_in(own_key, 6), axis_at), (blocks,), jnp.float32, smallest / len(split), top_value / len(split))
        gain = gain * jnp.repeat(jnp.exp(heights), extent[axis_at] // blocks).reshape((-1,) + (1,) * (len(extent) - 1 - axis_at))
    return gain


def normal_values(rng, dims, width, most, cuts=(), held_as=jnp.bfloat16):
    drawn = jax.random.normal(rng, dims, jnp.float32) * width
    if len(cuts) > 0:
        drawn = steps_of(rng, dims, cuts, -0.22, 0.18) * drawn
    return jnp.clip(drawn, min=-most, max=most).astype(held_as)


def setup_inputs(seed: int = 0) -> dict:
    keys = jax.random.split(jax.random.key(seed), 6)
    potential = normal_values(keys[0], (NX, NY, CZ), 16.0, 96.0, ((0, 4), (1, 8)), jnp.float32)
    gal_cells = plant(jax.random.randint(keys[1], (N_GX, N_YZ, N_YZ, CAP), 0, CX * CY), jax.random.fold_in(keys[1], 1), 0, (CX * CY) - 1).astype(jnp.int32)
    gal_z = plant(jax.random.randint(keys[2], (N_GX, N_YZ, N_YZ, CAP), 0, CZ), jax.random.fold_in(keys[2], 1), 0, CZ - 1).astype(jnp.int32)
    gal_bins = plant(jax.random.randint(keys[3], (N_GX, N_YZ, N_YZ, CAP), 0, BINS), jax.random.fold_in(keys[3], 1), 0, BINS - 1).astype(jnp.int32)
    gal_counts = draw_gal_counts(jax.random.fold_in(keys[5], 71), 0)
    return {"potential": potential, "gal_cells": gal_cells, "gal_z": gal_z, "gal_bins": gal_bins, "gal_counts": gal_counts}


def kernels():
    offsets = jnp.arange(-HALO, HALO + 1).astype(jnp.float32)
    sigma_cells = HALO / 3.0
    smooth_w = jnp.exp(-offsets * offsets / (2.0 * sigma_cells * sigma_cells))
    smooth_w = smooth_w / jnp.sum(smooth_w)
    first_w = offsets / (sigma_cells * sigma_cells) * smooth_w
    second_w = (offsets * offsets / sigma_cells ** 4 - 1.0 / (sigma_cells * sigma_cells)) * smooth_w
    return smooth_w, first_w, second_w


def sweep_axis(padded, weights, axis):
    length = padded.shape[axis] - 2 * HALO
    summed = weights[0] * lax.slice_in_dim(padded, 0, length, axis=axis)
    for k in range(1, 2 * HALO + 1):
        summed = summed + weights[k] * lax.slice_in_dim(padded, k, k + length, axis=axis)
    return summed


def plan_list(along_x, weights):
    x_smooth, x_first, x_second = along_x
    smooth_w, first_w, second_w = weights
    return [(x_second, smooth_w, smooth_w), (x_smooth, second_w, smooth_w), (x_smooth, smooth_w, second_w),
            (x_first, first_w, smooth_w), (x_first, smooth_w, first_w), (x_smooth, first_w, first_w)]


def one_component(field, y_w, z_w):
    in_y = sweep_axis(field, y_w, 1)
    wrapped = jnp.concatenate([in_y[:, :, -HALO:], in_y, in_y[:, :, :HALO]], axis=2)
    return sweep_axis(wrapped, z_w, 2)


def reference(potential, gal_cells, gal_z, gal_bins, gal_counts):
    weights = kernels()
    padded = jnp.pad(potential, ((HALO, HALO), (HALO, HALO), (0, 0)))
    along_x = [sweep_axis(padded, w, 0) for w in weights]
    scale = (HALO / 3.0) ** 2
    shape = gal_cells.shape
    band = lax.broadcasted_iota(jnp.int32, shape, 0)
    tile = lax.broadcasted_iota(jnp.int32, shape, 2)
    slot = lax.broadcasted_iota(jnp.int32, shape, 3)
    plane = gal_cells // CY
    row_in = gal_cells % CY
    z_index = gal_z
    x_global = band * CX + plane
    y_global = tile * CY + row_in
    z_next = (z_index + 1) % CZ
    weight = (gal_bins.astype(jnp.float32) + 0.5) / BINS
    live = slot < gal_counts[:, :, :, None]
    results = []
    for field, y_w, z_w in plan_list(along_x, weights):
        comp = one_component(field, y_w, z_w)
        here_value = comp[x_global, y_global, z_index]
        next_value = comp[x_global, y_global, z_next]
        value = ((1.0 - weight) * here_value + weight * next_value) * scale
        results.append(jnp.where(live, value, jnp.float32(0.0)))
    tidal = jnp.stack(results)
    return tidal.reshape(6, N_GX, N_YZ, N_YZ * CAP)
```

```python
import functools

import jax
import jax.numpy as jnp
import numpy as np
from jax import lax
from jax.experimental import pallas as pl
from jax.experimental.pallas import tpu as pltpu
from jax.sharding import PartitionSpec as P

HALO = 6
BINS = 8
LANES = 128
SUBS = 8
PARTS = 8
ALONG_X = (2, 0, 0, 1, 1, 0)
ALONG_Y = (0, 2, 0, 1, 0, 1)
ALONG_Z = (0, 0, 2, 0, 1, 1)


def taps():
    offsets = np.arange(-HALO, HALO + 1).astype(np.float32)
    sigma = np.float32(HALO / 3.0)
    smooth = np.exp(-offsets * offsets / (2 * sigma * sigma)).astype(np.float32)
    smooth = smooth / np.sum(smooth, dtype=np.float32)
    first = offsets / (sigma * sigma) * smooth
    second = (offsets * offsets / sigma**4 - 1 / (sigma * sigma)) * smooth
    return np.stack([smooth, first, second]).astype(np.float32)


def z_taps(rows):
    along = taps()
    table = np.zeros((2 * HALO + 1, 2, PARTS, rows), np.float32)
    for a, f in enumerate(ALONG_Z):
        table[:, :, a, :] = along[f][:, None, None]
    return table.reshape(2 * HALO + 1, LANES)


def x_table(planes, rows):
    along = taps()
    scale = np.float32((HALO / 3.0) ** 2)
    table = np.zeros((3 * planes, 2, planes // 2, 2, PARTS, rows), np.float32)
    for at in range(3 * planes):
        for x in range(planes):
            k = x - (at - planes)
            if abs(k) <= HALO:
                for a, f in enumerate(ALONG_X):
                    table[at, :, x // 2, x % 2, a, :] = along[f][k + HALO] * scale
    return table.reshape(3 * planes, SUBS, LANES)


def field_kernel(before, own, after, ztap, xtab, field, table, mid, turn, *, rows, depth):
    along = taps()
    ys = HALO
    per = depth // LANES

    upper = lax.broadcasted_iota(jnp.int32, (SUBS, LANES), 0) >= SUBS // 2
    for b in range(BINS):
        w = np.float32((b + 0.5) / BINS)
        cell_w = jnp.where(upper, w, np.float32(1.0) - w)
        for at in range(xtab.shape[0]):
            table[pl.ds((at * BINS + b) * SUBS, SUBS), :] = xtab[at] * cell_w

    def along_y(block, _):
        z0 = pl.multiple_of(block * LANES, LANES)
        zs = pl.ds(z0, LANES)
        u = [before[y, :, zs] for y in range(HALO)]
        u += [own[y, :, zs] for y in range(rows)]
        u += [after[y, :, zs] for y in range(HALO)]
        for r in range(rows):
            c = u[r + HALO]
            smooth = c * along[0][HALO]
            second = c * along[2][HALO]
            first = None
            for k in range(1, HALO + 1):
                up, down = u[r + HALO + k], u[r + HALO - k]
                both = up + down
                smooth = smooth + both * along[0][HALO + k]
                second = second + both * along[2][HALO + k]
                part = (up - down) * along[1][HALO + k]
                first = part if first is None else first + part
            for f, v in enumerate((smooth, first, second)):
                turn[pl.ds((f * rows + r) * SUBS, SUBS), :] = v
        for pair in range(SUBS // 2):
            tiles = []
            for half in range(2):
                x = 2 * pair + half
                by_filter = [turn[pl.ds(f * rows * SUBS + x, rows, stride=SUBS), :] for f in range(3)]
                tiles += [by_filter[ALONG_Y[a]] for a in range(6)] + [jnp.zeros_like(by_filter[0])] * 2
            flipped = jnp.concatenate(tiles, axis=0).T
            mid[pl.ds((z0 + SUBS) * 4 + pair, LANES, stride=4), :] = flipped
        return 0

    lax.fori_loop(0, per, along_y, 0)
    mid[pl.ds(0, 32), :] = mid[pl.ds(depth * 4, 32), :]
    mid[pl.ds((depth + SUBS) * 4, 32), :] = mid[pl.ds(32, 32), :]

    n = 8
    tap = [jnp.broadcast_to(ztap[k : k + 1, :], (SUBS, LANES)) for k in range(2 * HALO + 1)]

    def along_z(block, _):
        base = pl.multiple_of(block * (n * SUBS), n * SUBS)
        even = [mid[pl.ds(base + 8 + SUBS * j, SUBS), :] for j in range(n + 6)]
        odd = [mid[pl.ds(base + 12 + SUBS * j, SUBS), :] for j in range(n + 5)]
        for j in range(n):
            total = None
            for k in range(-HALO, HALO + 1):
                v = even[j + (k + HALO) // 2] if k % 2 == 0 else odd[j + (k + HALO) // 2]
                part = v * tap[k + HALO]
                total = part if total is None else total + part
            field[pl.ds(base + SUBS * j, SUBS), :] = total
        return 0

    lax.fori_loop(0, depth * 4 // (n * SUBS), along_z, 0)
    field[pl.ds(depth * 4, SUBS), :] = field[pl.ds(0, SUBS), :]


def lookup_kernel(words, place, rows_of, field, table, out, prod, *, bands, planes):
    me = place[0]
    homes = words.shape[0] // bands
    subs = lax.broadcasted_iota(jnp.int32, (SUBS, LANES), 0)

    def one_row(row, _):
        for j in range(LANES):
            word = words[row, j]
            at = (word & 0xFFFF) * 4
            w_at = pl.multiple_of((word >> 16) * SUBS, SUBS)
            prod[pl.ds(j * SUBS, SUBS), :] = field[pl.ds(at, SUBS), :] * table[pl.ds(w_at, SUBS), :]
        groups = []
        for i in range(LANES // SUBS):
            total = prod[pl.ds(i * SUBS * SUBS, SUBS, stride=SUBS), :]
            for s in range(1, SUBS):
                total = total + prod[pl.ds(i * SUBS * SUBS + s, SUBS, stride=SUBS), :]
            groups.append(total)
        flipped = jnp.concatenate(groups, axis=0).T
        mine = rows_of[pl.ds(row, 1), :] == subs
        for a in range(6):
            v = flipped[a * 8 : a * 8 + 8] + flipped[64 + a * 8 : 64 + a * 8 + 8]
            out[row, a, :] = jnp.sum(jnp.where(mine, v, 0.0), axis=0)
        return 0

    for band in range(bands):
        near = jnp.abs(band - me) <= 1

        @pl.when(near)
        def _():
            lax.fori_loop(band * homes, (band + 1) * homes, one_row, 0)

        @pl.when(jnp.logical_not(near))
        def _():
            out[pl.ds(band * homes, homes)] = jnp.zeros((homes, 6, LANES), jnp.float32)


def body(potential, gal_cells, gal_z, gal_bins, gal_counts):
    bands = lax.axis_size("gx")
    homes = lax.axis_size("yz")
    planes, rows, depth = potential.shape
    tiles, slots = gal_cells.shape[2:]
    assert planes == SUBS and rows == SUBS and slots == LANES
    vmem = pl.BlockSpec(memory_space=pltpu.VMEM)
    smem = pl.BlockSpec(memory_space=pltpu.SMEM)

    by_row = potential.transpose(1, 0, 2)
    up = [(i, i + 1) for i in range(homes - 1)]
    down = [(j, i) for i, j in up]
    before = lax.ppermute(by_row[rows - HALO :], "yz", up)
    after = lax.ppermute(by_row[:HALO], "yz", down)

    asked = jnp.concatenate([gal_cells, gal_z, gal_bins], axis=0).reshape(3, tiles, slots).transpose(1, 0, 2)
    asked = jnp.broadcast_to(asked[None], (bands, tiles, 3, slots)).reshape(bands * tiles, 3, slots)
    asked = lax.all_to_all(asked, ("gx", "yz"), split_axis=0, concat_axis=0, tiled=True)

    field, table = pl.pallas_call(
        functools.partial(field_kernel, rows=rows, depth=depth),
        out_shape=(
            jax.ShapeDtypeStruct((depth * 4 + SUBS, LANES), jnp.float32),
            jax.ShapeDtypeStruct((3 * planes * BINS * SUBS, LANES), jnp.float32),
        ),
        in_specs=[vmem] * 5,
        out_specs=(vmem, vmem),
        scratch_shapes=[
            pltpu.VMEM((depth * 4 + 8 * SUBS, LANES), jnp.float32),
            pltpu.VMEM((3 * rows * SUBS, LANES), jnp.float32),
        ],
    )(before, by_row, after, jnp.asarray(z_taps(rows)), jnp.asarray(x_table(planes, rows)))

    me = lax.axis_index("gx")
    band_of = lax.broadcasted_iota(jnp.int32, (bands * homes, slots), 0) // homes
    cells, zeds, bins = asked[:, 0], asked[:, 1], asked[:, 2]
    near = jnp.abs(band_of - me) <= 1
    at = jnp.where(near, (band_of - me + 1) * planes + cells // rows, 0)
    words = zeds + (at * BINS + bins) * 65536
    served = pl.pallas_call(
        functools.partial(lookup_kernel, bands=bands, planes=planes),
        out_shape=jax.ShapeDtypeStruct((bands * homes, 6, slots), jnp.float32),
        in_specs=[smem, smem, vmem, vmem, vmem],
        out_specs=vmem,
        scratch_shapes=[pltpu.VMEM((LANES * SUBS, LANES), jnp.float32)],
    )(words, me.reshape(1), cells % rows, field, table)

    returned = lax.all_to_all(served, ("gx", "yz"), split_axis=0, concat_axis=0, tiled=True)
    total = jnp.sum(returned.reshape(bands, tiles, 6, slots), axis=0)
    slot_index = lax.broadcasted_iota(jnp.int32, (tiles, slots), 1)
    live = slot_index < gal_counts.reshape(tiles, 1)
    tidal = jnp.where(live[None], total.transpose(1, 0, 2), jnp.float32(0.0))
    return tidal.reshape(6, 1, 1, tiles * slots)


def solution(mesh):
    return jax.shard_map(
        body,
        mesh=mesh,
        in_specs=(
            P("gx", "yz", None),
            P("gx", "yz", None, None),
            P("gx", "yz", None, None),
            P("gx", "yz", None, None),
            P("gx", "yz", None),
        ),
        out_specs=P(None, "gx", "yz", None),
        check_vma=False,
    )
```

```python
import functools

import jax
import jax.numpy as jnp
import numpy as np
from jax import lax
from jax.experimental import pallas as pl
from jax.experimental.pallas import tpu as pltpu
from jax.sharding import PartitionSpec as P


HALO = 6
BINS = 8
LANES = 128
SUBS = 8
PARTS = 8
ALONG_X = (2, 0, 0, 1, 1, 0)
ALONG_Y = (0, 2, 0, 1, 0, 1)
ALONG_Z = (0, 0, 2, 0, 1, 1)


def taps():
    offsets = np.arange(-HALO, HALO + 1).astype(np.float32)
    sigma = np.float32(HALO / 3.0)
    smooth = np.exp(-offsets * offsets / (2 * sigma * sigma)).astype(np.float32)
    smooth = smooth / np.sum(smooth, dtype=np.float32)
    first = offsets / (sigma * sigma) * smooth
    second = (offsets * offsets / sigma**4 - 1 / (sigma * sigma)) * smooth
    return np.stack([smooth, first, second]).astype(np.float32)


def spread(along, values):
    part = lax.broadcasted_iota(jnp.int32, (SUBS, LANES), 1) // SUBS % PARTS
    out = jnp.full((SUBS, LANES), values[along[0]], jnp.float32)
    for a in range(1, len(along)):
        if along[a] != along[0]:
            out = jnp.where(part == a, values[along[a]], out)
    return out


def field_kernel(before, own, after, field, mid, flip, turn, done, sent, *, rows, depth, chunks):
    along = taps()
    blocks = depth // LANES
    odd_sign = spread(ALONG_Z, (1.0, -1.0, 1.0))

    def along_y(block, slot):
        zs = pl.ds(pl.multiple_of(block * LANES, LANES), LANES)
        u = [before[y, :, zs] for y in range(HALO)]
        u += [own[y, :, zs] for y in range(rows)]
        u += [after[y, :, zs] for y in range(HALO)]
        for r in range(rows):
            c = u[r + HALO]
            smooth = c * along[0][HALO]
            second = c * along[2][HALO]
            first = None
            for k in range(1, HALO + 1):
                up, down = u[r + HALO + k], u[r + HALO - k]
                both = up + down
                smooth = smooth + both * along[0][HALO + k]
                second = second + both * along[2][HALO + k]
                part = (up - down) * along[1][HALO + k]
                first = part if first is None else first + part
            for f, v in enumerate((smooth, first, second)):
                turn[slot, pl.ds((f * rows + r) * SUBS, SUBS), :] = v

    def transpose(block, slot):
        base = pl.multiple_of(block * (LANES * 4), LANES * 4) + SUBS * 4
        for pair in range(SUBS // 2):
            tiles = []
            for half in range(2):
                x = 2 * pair + half
                by_filter = [turn[slot, pl.ds(f * rows * SUBS + x, rows, stride=SUBS), :] for f in range(3)]
                tiles += [by_filter[ALONG_Y[a]] for a in range(6)] + [by_filter[0]] * 2
            flipped = jnp.concatenate(tiles, axis=0).T
            mid[pl.ds(base + pair, LANES, stride=4), :] = flipped
            signed = flipped.reshape(LANES // SUBS, SUBS, LANES) * odd_sign
            flip[pl.ds(base + pair, LANES, stride=4), :] = signed.reshape(LANES, LANES)

    along_y(0, 0)

    def two_blocks(i, _):
        along_y(2 * i + 1, 1)
        transpose(2 * i, 0)
        along_y(2 * i + 2, 0)
        transpose(2 * i + 1, 1)
        return 0

    lax.fori_loop(0, blocks // 2 - 1, two_blocks, 0)
    along_y(blocks - 1, 1)
    transpose(blocks - 2, 0)
    transpose(blocks - 1, 1)
    for buf in (mid, flip):
        buf[pl.ds(0, 32), :] = buf[pl.ds(depth * 4, 32), :]
        buf[pl.ds((depth + SUBS) * 4, 32), :] = buf[pl.ds(32, 32), :]

    n = 16
    tap = [spread(ALONG_Z, along[:, k + HALO]) for k in range(HALO + 1)]
    size = depth * 4 // chunks
    steps = size // (n * SUBS)

    def along_z(block, _):
        base = pl.multiple_of(block * (n * SUBS), n * SUBS)
        for j in range(n):
            at = base + SUBS * j + 32
            total = mid[pl.ds(at, SUBS), :] * tap[0]
            for k in range(1, HALO + 1):
                total = total + (mid[pl.ds(at + 4 * k, SUBS), :] + flip[pl.ds(at - 4 * k, SUBS), :]) * tap[k]
            done[pl.ds(base + SUBS * j, SUBS), :] = total
        return 0

    def send(c):
        part = pl.ds(pl.multiple_of(c * size, size), size)
        return pltpu.make_async_copy(done.at[part], field.at[part], sent.at[c])

    wrap = pltpu.make_async_copy(done.at[pl.ds(0, SUBS)], field.at[pl.ds(depth * 4, SUBS)], sent.at[chunks])

    def one_chunk(c, _):
        lax.fori_loop(c * steps, (c + 1) * steps, along_z, 0)
        send(c).start()
        return 0

    lax.fori_loop(0, chunks, one_chunk, 0)
    wrap.start()
    for c in range(chunks):
        send(c).wait()
    wrap.wait()


def fill_table(table, planes):
    along = taps()
    scale = np.float32((HALO / 3.0) ** 2)
    sub = lax.broadcasted_iota(jnp.int32, (SUBS, LANES), 0)
    lane = lax.broadcasted_iota(jnp.int32, (SUBS, LANES), 1)
    upper = sub >= SUBS // 2
    plane = sub % (SUBS // 2) * 2 + lane // (LANES // 2)
    x_tap = [spread(ALONG_X, along[:, k] * scale) for k in range(2 * HALO + 1)]
    for at in range(3 * planes):
        weight = jnp.zeros((SUBS, LANES), jnp.float32)
        for k in range(-HALO, HALO + 1):
            if 0 <= at - planes + k < planes:
                weight = jnp.where(plane == at - planes + k, x_tap[k + HALO], weight)
        for b in range(BINS):
            w = np.float32((b + 0.5) / BINS)
            table[pl.ds((at * BINS + b) * SUBS, SUBS), :] = weight * jnp.where(upper, w, np.float32(1.0) - w)


def lookup_kernel(
    place, asked, field_hbm, out, field, table, prod, at_v, table_at_v, rows_of, at_s, table_at_s, sent, *, bands, planes, rows
):
    me = place[0]
    homes = asked.shape[0] // bands
    subs = lax.broadcasted_iota(jnp.int32, (SUBS, LANES), 0)
    fetch = pltpu.make_async_copy(field_hbm, field, sent.at[0])
    fetch.start()

    def read_row(row, _):
        cell, z, b = asked[row, 0:1, :], asked[row, 1:2, :], asked[row, 2:3, :]
        band = row // homes
        at = jnp.where(cell >= 0, (band - me + 1) * planes + cell // rows, 0)
        at_v[pl.ds(row, 1), :] = z * 4
        table_at_v[pl.ds(row, 1), :] = (at * BINS + b) * SUBS
        rows_of[pl.ds(row, 1), :] = cell % rows
        return 0

    lax.fori_loop(0, bands * homes, read_row, 0, unroll=4)
    moves = [pltpu.make_async_copy(at_v, at_s, sent.at[1]), pltpu.make_async_copy(table_at_v, table_at_s, sent.at[2])]
    for move in moves:
        move.start()
    fill_table(table, planes)
    for move in moves:
        move.wait()
    fetch.wait()

    def multiply(row, slot):
        for j in range(LANES):
            w_at = pl.multiple_of(table_at_s[row, j], SUBS)
            prod[slot, pl.ds(j * SUBS, SUBS), :] = field[pl.ds(at_s[row, j], SUBS), :] * table[pl.ds(w_at, SUBS), :]

    def reduce(row, slot):
        groups = []
        for i in range(LANES // SUBS):
            total = prod[slot, pl.ds(i * SUBS * SUBS, SUBS, stride=SUBS), :]
            for s in range(1, SUBS):
                total = total + prod[slot, pl.ds(i * SUBS * SUBS + s, SUBS, stride=SUBS), :]
            groups.append(total)
        flipped = jnp.concatenate(groups, axis=0).T
        mine = rows_of[pl.ds(row, 1), :] == subs
        for a in range(6):
            v = flipped[a * 8 : a * 8 + 8] + flipped[64 + a * 8 : 64 + a * 8 + 8]
            out[row, a, :] = jnp.sum(jnp.where(mine, v, 0.0), axis=0)

    first = jnp.maximum(me - 1, 0) * homes
    last = jnp.minimum(me + 2, bands) * homes

    def no_row(row, _):
        out[row] = jnp.zeros((6, LANES), jnp.float32)
        return 0

    lax.fori_loop(0, first, no_row, 0)

    multiply(first, 0)

    def two_rows(i, _):
        row = first + 2 * i
        multiply(row + 1, 1)
        reduce(row, 0)
        multiply(jnp.minimum(row + 2, last - 1), 0)
        reduce(row + 1, 1)
        return 0

    lax.fori_loop(0, (last - first) // 2, two_rows, 0)
    lax.fori_loop(last, bands * homes, no_row, 0)


def in_vmem(x):
    return pltpu.with_memory_space_constraint(x, pltpu.VMEM)


def body(potential, gal_cells, gal_z, gal_bins, gal_counts):
    bands = lax.axis_size("gx")
    homes = lax.axis_size("yz")
    planes, rows, depth = potential.shape
    tiles, slots = gal_cells.shape[2:]
    assert planes == SUBS and rows == SUBS and slots == LANES and homes % 2 == 0
    vmem = pl.BlockSpec(memory_space=pltpu.VMEM)
    smem = pl.BlockSpec(memory_space=pltpu.SMEM)

    by_row = potential.transpose(1, 0, 2)
    up = [(i, i + 1) for i in range(homes - 1)]
    down = [(j, i) for i, j in up]
    before = lax.ppermute(by_row[rows - HALO :], "yz", up)
    after = lax.ppermute(by_row[:HALO], "yz", down)

    slot_index = lax.broadcasted_iota(jnp.int32, (1, 1, tiles, slots), 3)
    gal_cells = jnp.where(slot_index < gal_counts[..., None], gal_cells, -1)
    asked = jnp.concatenate([gal_cells, gal_z, gal_bins], axis=0).reshape(3, tiles, slots).transpose(1, 0, 2)
    asked = jnp.broadcast_to(asked[None], (bands, tiles, 3, slots)).reshape(bands * tiles, 3, slots)
    asked = lax.all_to_all(asked, ("gx", "yz"), split_axis=0, concat_axis=0, tiled=True)

    chunks = 8
    field_shape = (depth * 4 + SUBS, LANES)
    mid_shape = (depth * 4 + 8 * SUBS, LANES)
    hbm = pl.BlockSpec(memory_space=pltpu.HBM)
    field = pl.pallas_call(
        functools.partial(field_kernel, rows=rows, depth=depth, chunks=chunks),
        out_shape=pltpu.HBM(field_shape, jnp.float32),
        in_specs=[vmem] * 3,
        out_specs=hbm,
        scratch_shapes=[
            pltpu.VMEM(mid_shape, jnp.float32),
            pltpu.VMEM(mid_shape, jnp.float32),
            pltpu.VMEM((2, 3 * rows * SUBS, LANES), jnp.float32),
            pltpu.VMEM(field_shape, jnp.float32),
            pltpu.SemaphoreType.DMA((chunks + 1,)),
        ],
        compiler_params=pltpu.CompilerParams(vmem_limit_bytes=24 << 20),
    )(in_vmem(before), in_vmem(by_row), in_vmem(after))

    me = lax.axis_index("gx")
    queries = (bands * homes, slots)
    served = pl.pallas_call(
        functools.partial(lookup_kernel, bands=bands, planes=planes, rows=rows),
        out_shape=jax.ShapeDtypeStruct((bands * homes, 6, slots), jnp.float32),
        in_specs=[smem, vmem, hbm],
        out_specs=vmem,
        scratch_shapes=[
            pltpu.VMEM(field_shape, jnp.float32),
            pltpu.VMEM((3 * planes * BINS * SUBS, LANES), jnp.float32),
            pltpu.VMEM((2, LANES * SUBS, LANES), jnp.float32),
            pltpu.VMEM(queries, jnp.int32),
            pltpu.VMEM(queries, jnp.int32),
            pltpu.VMEM(queries, jnp.int32),
            pltpu.SMEM(queries, jnp.int32),
            pltpu.SMEM(queries, jnp.int32),
            pltpu.SemaphoreType.DMA((3,)),
        ],
        compiler_params=pltpu.CompilerParams(vmem_limit_bytes=24 << 20),
    )(me.reshape(1), asked, pltpu.with_memory_space_constraint(field, pltpu.HBM))

    returned = lax.all_to_all(served, ("gx", "yz"), split_axis=0, concat_axis=0, tiled=True)
    total = jnp.sum(returned.reshape(bands, tiles, 6, slots), axis=0)
    return total.transpose(1, 0, 2).reshape(6, 1, 1, tiles * slots)


def solution(mesh):
    return jax.shard_map(
        body,
        mesh=mesh,
        in_specs=(
            P("gx", "yz", None),
            P("gx", "yz", None, None),
            P("gx", "yz", None, None),
            P("gx", "yz", None, None),
            P("gx", "yz", None),
        ),
        out_specs=P(None, "gx", "yz", None),
        check_vma=False,
    )
```

```python
import functools

import jax
import jax.numpy as jnp
import numpy as np
from jax import lax
from jax.experimental import pallas as pl
from jax.experimental.pallas import tpu as pltpu
from jax.sharding import PartitionSpec as P


HALO = 6
BINS = 8
LANES = 128
SUBS = 8
CELL = 3
HELD = ((0, 3), (4, 5), (2, 1))
ALONG_X = (2, 0, 0, 1, 1, 0)


def taps():
    offsets = np.arange(-HALO, HALO + 1).astype(np.float32)
    sigma = np.float32(HALO / 3.0)
    smooth = np.exp(-offsets * offsets / (2 * sigma * sigma)).astype(np.float32)
    smooth = smooth / np.sum(smooth, dtype=np.float32)
    first = offsets / (sigma * sigma) * smooth
    second = (offsets * offsets / sigma**4 - 1 / (sigma * sigma)) * smooth
    return np.stack([smooth, first, second]).astype(np.float32)


def send_kernel(
    parity, counts_in, cells_in, zeds_in, bins_in, own_in, pair_out, next_out, asked_out, hold,
    counts, cells, zeds, bins, own, asked, came, gone, *, bands, rows
):
    fetches = [pltpu.make_async_copy(own_in.at[x], own.at[x], came.at[x]) for x in range(own.shape[0])]
    small = ((counts_in, counts), (cells_in, cells), (zeds_in, zeds), (bins_in, bins))
    small = [pltpu.make_async_copy(a, b, came.at[own.shape[0] + i]) for i, (a, b) in enumerate(small)]
    for copy in small + fetches:
        copy.start()
    for copy in small:
        copy.wait()
    tiles, slots = cells.shape
    slot = lax.broadcasted_iota(jnp.int32, (1, slots), 1)
    for t in range(tiles):
        cell = jnp.where(slot < counts[0, t], cells[t : t + 1, :], -1)
        query = jnp.concatenate([cell, zeds[t : t + 1, :], bins[t : t + 1, :]], axis=0)
        for band in range(bands):
            asked[band * tiles + t] = query
    moves = [pltpu.make_async_copy(asked, asked_out, gone.at[2, 0])]
    moves[0].start()
    for copy in fetches:
        copy.wait()
    to_pair = (rows - HALO) * (1 - parity[0])
    to_next = (rows - HALO) * parity[0]
    for y in range(HALO):
        moves.append(pltpu.make_async_copy(own.at[:, to_pair + y, :], pair_out.at[y], gone.at[0, y]))
        moves.append(pltpu.make_async_copy(own.at[:, to_next + y, :], next_out.at[y], gone.at[1, y]))
    for copy in moves[1:]:
        copy.start()
    for copy in moves:
        copy.wait()


def field_kernel(parity, pair_in, own_in, next_in, hold, field, before, after, own, mid_01, mid_02, came, *, rows, depth, chunks):
    along = taps()
    size = depth // chunks
    per = size // LANES
    planes = own_in.shape[0]

    def fetches(c, pair_to, next_to):
        zs = pl.ds(c * size, size)
        return [
            pltpu.make_async_copy(pair_in.at[:, :, zs], pair_to.at[:, :, zs], came.at[c, 0]),
            pltpu.make_async_copy(next_in.at[:, :, zs], next_to.at[:, :, zs], came.at[c, 1]),
        ] + [pltpu.make_async_copy(own_in.at[x, :, zs], own.at[:, x, zs], came.at[c, 2 + x]) for x in range(planes)]

    even = parity[0] == 0
    for c in range(chunks):
        for copy in fetches(c, after, before)[2:]:
            copy.start()

        @pl.when(even)
        def _():
            for copy in fetches(c, after, before)[:2]:
                copy.start()

        @pl.when(jnp.logical_not(even))
        def _():
            for copy in fetches(c, before, after)[:2]:
                copy.start()

    def along_y(block, _):
        z0 = pl.multiple_of(block * LANES, LANES)
        zs = pl.ds(z0, LANES)
        u = [before[y, :, zs] for y in range(HALO)]
        u += [own[y, :, zs] for y in range(rows)]
        u += [after[y, :, zs] for y in range(HALO)]
        filtered = [[], [], []]
        for r in range(rows):
            c = u[r + HALO]
            smooth = c * along[0][HALO]
            second = c * along[2][HALO]
            first = None
            for k in range(1, HALO + 1):
                up, down = u[r + HALO + k], u[r + HALO - k]
                both = up + down
                smooth = smooth + both * along[0][HALO + k]
                second = second + both * along[2][HALO + k]
                part = (up - down) * along[1][HALO + k]
                first = part if first is None else first + part
            for f, v in enumerate((smooth, first, second)):
                filtered[f].append(v)
        mid_01[pl.ds(z0 + SUBS, LANES), :] = jnp.concatenate(filtered[0] + filtered[1], axis=0).T
        mid_02[pl.ds(z0 + SUBS, LANES), :] = jnp.concatenate(filtered[0] + filtered[2], axis=0).T
        return 0

    for c in range(chunks):
        for copy in fetches(c, after, before):
            copy.wait()
        lax.fori_loop(c * per, (c + 1) * per, along_y, 0, unroll=2)
    for buf in (mid_01, mid_02):
        buf[pl.ds(0, SUBS), :] = buf[pl.ds(depth, SUBS), :]
        buf[pl.ds(depth + SUBS, SUBS), :] = buf[pl.ds(SUBS, SUBS), :]

    n = 8
    lower = lax.broadcasted_iota(jnp.int32, (SUBS, LANES), 1) < LANES // 2
    mixed = [jnp.where(lower, along[2][HALO + k], along[0][HALO + k]) for k in range(HALO + 1)]

    def along_z(block, _):
        base = pl.multiple_of(block * (n * SUBS), n * SUBS)
        for j in range(n):
            at = base + SUBS * j + SUBS
            smooth = mid_01[pl.ds(at, SUBS), :] * along[0][HALO]
            first = None
            both = mid_02[pl.ds(at, SUBS), :] * mixed[0]
            for k in range(1, HALO + 1):
                up, down = mid_01[pl.ds(at + k, SUBS), :], mid_01[pl.ds(at - k, SUBS), :]
                smooth = smooth + (up + down) * along[0][HALO + k]
                part = (up - down) * along[1][HALO + k]
                first = part if first is None else first + part
                up, down = mid_02[pl.ds(at + k, SUBS), :], mid_02[pl.ds(at - k, SUBS), :]
                both = both + (up + down) * mixed[k]
            for i, v in enumerate((smooth, first, both)):
                field[pl.ds((base + SUBS * j) * CELL + i, SUBS, stride=CELL), :] = v
        return 0

    lax.fori_loop(0, depth // (n * SUBS), along_z, 0)
    field[pl.ds(depth * CELL, SUBS), :] = field[pl.ds(0, SUBS), :]


def fill_table(table, planes):
    along = taps()
    scale = np.float32((HALO / 3.0) ** 2)
    sub = lax.broadcasted_iota(jnp.int32, (SUBS, LANES), 0)
    lane = lax.broadcasted_iota(jnp.int32, (SUBS, LANES), 1)
    plane = lane % planes
    half = lane // (LANES // 2)

    def x_tap(k):
        out = jnp.zeros((SUBS, LANES), jnp.float32)
        for i, pair in enumerate(HELD):
            for h, a in enumerate(pair):
                held = ((sub == i) | (sub == i + CELL)) & (half == h)
                out = jnp.where(held, along[ALONG_X[a]][k + HALO] * scale, out)
        return out

    x_taps = [x_tap(k) for k in range(-HALO, HALO + 1)]
    for at in range(3 * planes):
        weight = jnp.zeros((SUBS, LANES), jnp.float32)
        for k in range(-HALO, HALO + 1):
            if 0 <= at - planes + k < planes:
                weight = jnp.where(plane == at - planes + k, x_taps[k + HALO], weight)
        for b in range(BINS):
            w = np.float32((b + 0.5) / BINS)
            table[pl.ds((at * BINS + b) * SUBS, SUBS), :] = weight * jnp.where(sub >= CELL, w, np.float32(1.0) - w)


def woven(many, few):
    each = max(len(many) // max(len(few), 1), 1)
    few = list(few)
    for i, step in enumerate(many):
        if i % each == 0 and few:
            few.pop(0)()
        step()
    for step in few:
        step()


def lookup_kernel(
    place, asked, field, out, table, prod, sums, at_v, table_at_v, rows_of, at_s, table_at_s, sent, *, bands, planes, rows
):
    me = place[0]
    homes = asked.shape[0] // bands

    def read_row(row, _):
        cell, z, b = asked[row, 0:1, :], asked[row, 1:2, :], asked[row, 2:3, :]
        band = row // homes
        at = jnp.where(cell >= 0, (band - me + 1) * planes + cell // rows, 0)
        at_v[pl.ds(row, 1), :] = z * CELL
        table_at_v[pl.ds(row, 1), :] = (at * BINS + b) * SUBS
        rows_of[pl.ds(row, 1), :] = cell % rows
        return 0

    lax.fori_loop(0, bands * homes, read_row, 0, unroll=4)
    moves = [pltpu.make_async_copy(at_v, at_s, sent.at[0]), pltpu.make_async_copy(table_at_v, table_at_s, sent.at[1])]
    for move in moves:
        move.start()
    fill_table(table, planes)
    for move in moves:
        move.wait()

    def multiply(row, slot):
        def one_group(i):
            for j in range(i * SUBS, (i + 1) * SUBS):
                w_at = pl.multiple_of(table_at_s[row, j], SUBS)
                prod[slot, pl.ds(j * SUBS, SUBS), :] = field[pl.ds(at_s[row, j], SUBS), :] * table[pl.ds(w_at, SUBS), :]

        return [functools.partial(one_group, i) for i in range(LANES // SUBS)]

    def reduce(slot):
        def one_group(i):
            for c in range(CELL):
                here = prod[slot, pl.ds(i * SUBS * SUBS + c, SUBS, stride=SUBS), :]
                beyond = prod[slot, pl.ds(i * SUBS * SUBS + CELL + c, SUBS, stride=SUBS), :]
                sums[slot, c, pl.ds(i * SUBS, SUBS), :] = here + beyond

        return [functools.partial(one_group, i) for i in range(LANES // SUBS)]

    def finish(row, slot):
        mine = jnp.broadcast_to(rows_of[pl.ds(row, 1), :], (SUBS, LANES))
        for c, pair in enumerate(HELD):
            flipped = sums[slot, c].T
            for h, a in enumerate(pair):
                at = h * rows * SUBS
                picked = flipped[at : at + SUBS]
                for r in range(1, rows):
                    picked = jnp.where(mine == r, flipped[at + r * SUBS : at + (r + 1) * SUBS], picked)
                out[row, a, :] = jnp.sum(picked, axis=0)

    first = jnp.maximum(me - 1, 0) * homes
    last = jnp.minimum(me + 2, bands) * homes

    def no_row(row, _):
        out[row] = jnp.zeros((6, LANES), jnp.float32)
        return 0

    lax.fori_loop(0, first, no_row, 0)

    sums[1] = jnp.zeros((CELL, LANES, LANES), jnp.float32)
    woven(multiply(first, 0), [])

    def two_rows(i, _):
        row = first + 2 * i
        finish(jnp.maximum(row - 1, first), 1)
        woven(multiply(row + 1, 1), reduce(0))
        finish(row, 0)
        woven(multiply(jnp.minimum(row + 2, last - 1), 0), reduce(1))
        return 0

    lax.fori_loop(0, (last - first) // 2, two_rows, 0)
    finish(last - 1, 1)
    lax.fori_loop(last, bands * homes, no_row, 0)


def in_hbm(x):
    return pltpu.with_memory_space_constraint(x, pltpu.HBM)


def in_vmem(x):
    return pltpu.with_memory_space_constraint(x, pltpu.VMEM)


def body(potential, gal_cells, gal_z, gal_bins, gal_counts):
    bands = lax.axis_size("gx")
    homes = lax.axis_size("yz")
    planes, rows, depth = potential.shape
    tiles, slots = gal_cells.shape[2:]
    assert planes == SUBS and rows == SUBS and slots == LANES and homes % 2 == 0
    vmem = pl.BlockSpec(memory_space=pltpu.VMEM)
    smem = pl.BlockSpec(memory_space=pltpu.SMEM)

    parity = (lax.axis_index("yz") % 2).reshape(1)
    hbm = pl.BlockSpec(memory_space=pltpu.HBM)
    field_shape = (depth * CELL + SUBS, LANES)
    halo_shape = (HALO, planes, depth)
    pair_out, next_out, asked, hold = pl.pallas_call(
        functools.partial(send_kernel, bands=bands, rows=rows),
        out_shape=(
            jax.ShapeDtypeStruct(halo_shape, jnp.float32),
            jax.ShapeDtypeStruct(halo_shape, jnp.float32),
            jax.ShapeDtypeStruct((bands * tiles, 3, slots), jnp.int32),
            pltpu.VMEM(field_shape, jnp.float32),
        ),
        in_specs=[smem] + [hbm] * 5,
        out_specs=(hbm, hbm, hbm, vmem),
        scratch_shapes=[
            pltpu.SMEM((1, tiles), jnp.int32),
            pltpu.VMEM((tiles, slots), jnp.int32),
            pltpu.VMEM((tiles, slots), jnp.int32),
            pltpu.VMEM((tiles, slots), jnp.int32),
            pltpu.VMEM(potential.shape, jnp.float32),
            pltpu.VMEM((bands * tiles, 3, slots), jnp.int32),
            pltpu.SemaphoreType.DMA((planes + 4,)),
            pltpu.SemaphoreType.DMA((3, HALO)),
        ],
        compiler_params=pltpu.CompilerParams(vmem_limit_bytes=8 << 20),
    )(
        parity,
        in_hbm(gal_counts.reshape(1, tiles)),
        in_hbm(gal_cells.reshape(tiles, slots)),
        in_hbm(gal_z.reshape(tiles, slots)),
        in_hbm(gal_bins.reshape(tiles, slots)),
        in_hbm(potential),
    )

    swap = lambda first: [p for i in range(first, homes - 1, 2) for p in ((i, i + 1), (i + 1, i))]
    pair_in = lax.ppermute(pair_out, "yz", swap(0))
    next_in = lax.ppermute(next_out, "yz", swap(1))
    asked = lax.all_to_all(asked, ("gx", "yz"), split_axis=0, concat_axis=0, tiled=True)

    chunks = 4
    mid_shape = (depth + 2 * SUBS, LANES)
    field = pl.pallas_call(
        functools.partial(field_kernel, rows=rows, depth=depth, chunks=chunks),
        out_shape=pltpu.VMEM(field_shape, jnp.float32),
        in_specs=[smem, hbm, hbm, hbm, vmem],
        out_specs=vmem,
        input_output_aliases={4: 0},
        scratch_shapes=[
            pltpu.VMEM(halo_shape, jnp.float32),
            pltpu.VMEM(halo_shape, jnp.float32),
            pltpu.VMEM((rows, planes, depth), jnp.float32),
            pltpu.VMEM(mid_shape, jnp.float32),
            pltpu.VMEM(mid_shape, jnp.float32),
            pltpu.SemaphoreType.DMA((chunks, 2 + planes)),
        ],
        compiler_params=pltpu.CompilerParams(vmem_limit_bytes=24 << 20),
    )(parity, in_hbm(pair_in), in_hbm(potential), in_hbm(next_in), in_vmem(hold))

    me = lax.axis_index("gx")
    queries = (bands * homes, slots)
    served = pl.pallas_call(
        functools.partial(lookup_kernel, bands=bands, planes=planes, rows=rows),
        out_shape=jax.ShapeDtypeStruct((bands * homes, 6, slots), jnp.float32),
        in_specs=[smem, vmem, vmem],
        out_specs=vmem,
        scratch_shapes=[
            pltpu.VMEM((3 * planes * BINS * SUBS, LANES), jnp.float32),
            pltpu.VMEM((2, LANES * SUBS + SUBS, LANES), jnp.float32),
            pltpu.VMEM((2, CELL, LANES, LANES), jnp.float32),
            pltpu.VMEM(queries, jnp.int32),
            pltpu.VMEM(queries, jnp.int32),
            pltpu.VMEM(queries, jnp.int32),
            pltpu.SMEM(queries, jnp.int32),
            pltpu.SMEM(queries, jnp.int32),
            pltpu.SemaphoreType.DMA((2,)),
        ],
        compiler_params=pltpu.CompilerParams(vmem_limit_bytes=24 << 20),
    )(me.reshape(1), asked, in_vmem(field))

    returned = lax.all_to_all(served, ("gx", "yz"), split_axis=0, concat_axis=0, tiled=True)
    total = jnp.sum(returned.reshape(bands, tiles, 6, slots), axis=0)
    return total.transpose(1, 0, 2).reshape(6, 1, 1, tiles * slots)


def solution(mesh):
    return jax.shard_map(
        body,
        mesh=mesh,
        in_specs=(
            P("gx", "yz", None),
            P("gx", "yz", None, None),
            P("gx", "yz", None, None),
            P("gx", "yz", None, None),
            P("gx", "yz", None),
        ),
        out_specs=P(None, "gx", "yz", None),
        check_vma=False,
    )
```

```python
import functools

import jax
import jax.numpy as jnp
import numpy as np
from jax import lax
from jax.experimental import pallas as pl
from jax.experimental.pallas import tpu as pltpu
from jax.sharding import PartitionSpec as P


HALO = 6
BINS = 8
LANES = 128
SUBS = 8
UNROLL = 4
CELL = 3
HELD = ((0, 3), (4, 5), (2, 1))
ALONG_X = (2, 0, 0, 1, 1, 0)


def taps():
    offsets = np.arange(-HALO, HALO + 1).astype(np.float32)
    sigma = np.float32(HALO / 3.0)
    smooth = np.exp(-offsets * offsets / (2 * sigma * sigma)).astype(np.float32)
    smooth = smooth / np.sum(smooth, dtype=np.float32)
    first = offsets / (sigma * sigma) * smooth
    second = (offsets * offsets / sigma**4 - 1 / (sigma * sigma)) * smooth
    return np.stack([smooth, first, second]).astype(np.float32)


def send_kernel(
    parity, counts_in, cells_in, zeds_in, bins_in, own_in, pair_out, next_out, asked_out, hold,
    counts, cells, zeds, bins, own, asked, came, gone, *, bands, rows
):
    fetches = [pltpu.make_async_copy(own_in.at[x], own.at[x], came.at[x]) for x in range(own.shape[0])]
    small = ((counts_in, counts), (cells_in, cells), (zeds_in, zeds), (bins_in, bins))
    small = [pltpu.make_async_copy(a, b, came.at[own.shape[0] + i]) for i, (a, b) in enumerate(small)]
    for copy in small + fetches:
        copy.start()
    for copy in small:
        copy.wait()
    tiles, slots = cells.shape
    slot = lax.broadcasted_iota(jnp.int32, (1, slots), 1)
    for t in range(tiles):
        cell = jnp.where(slot < counts[0, t], cells[t : t + 1, :], -1)
        query = jnp.concatenate([cell, zeds[t : t + 1, :], bins[t : t + 1, :]], axis=0)
        for band in range(bands):
            asked[band * tiles + t] = query
    moves = [pltpu.make_async_copy(asked, asked_out, gone.at[2, 0])]
    moves[0].start()
    for copy in fetches:
        copy.wait()
    to_pair = (rows - HALO) * (1 - parity[0])
    to_next = (rows - HALO) * parity[0]
    for y in range(HALO):
        moves.append(pltpu.make_async_copy(own.at[:, to_pair + y, :], pair_out.at[y], gone.at[0, y]))
        moves.append(pltpu.make_async_copy(own.at[:, to_next + y, :], next_out.at[y], gone.at[1, y]))
    for copy in moves[1:]:
        copy.start()
    for copy in moves:
        copy.wait()


def field_kernel(parity, pair_in, own_in, next_in, hold, field, before, after, own, mid_01, mid_02, came, *, rows, depth, chunks):
    along = taps()
    size = depth // chunks
    per = size // LANES
    planes = own_in.shape[0]

    def fetches(c, pair_to, next_to):
        zs = pl.ds(c * size, size)
        return [
            pltpu.make_async_copy(pair_in.at[:, :, zs], pair_to.at[:, :, zs], came.at[c, 0]),
            pltpu.make_async_copy(next_in.at[:, :, zs], next_to.at[:, :, zs], came.at[c, 1]),
        ] + [pltpu.make_async_copy(own_in.at[x, :, zs], own.at[:, x, zs], came.at[c, 2 + x]) for x in range(planes)]

    even = parity[0] == 0
    for c in range(chunks):
        for copy in fetches(c, after, before)[2:]:
            copy.start()

        @pl.when(even)
        def _():
            for copy in fetches(c, after, before)[:2]:
                copy.start()

        @pl.when(jnp.logical_not(even))
        def _():
            for copy in fetches(c, before, after)[:2]:
                copy.start()

    def along_y(block, _):
        z0 = pl.multiple_of(block * LANES, LANES)
        zs = pl.ds(z0, LANES)
        u = [before[y, :, zs] for y in range(HALO)]
        u += [own[y, :, zs] for y in range(rows)]
        u += [after[y, :, zs] for y in range(HALO)]
        filtered = [[], [], []]
        for r in range(rows):
            c = u[r + HALO]
            smooth = c * along[0][HALO]
            second = c * along[2][HALO]
            first = None
            for k in range(1, HALO + 1):
                up, down = u[r + HALO + k], u[r + HALO - k]
                both = up + down
                smooth = smooth + both * along[0][HALO + k]
                second = second + both * along[2][HALO + k]
                part = (up - down) * along[1][HALO + k]
                first = part if first is None else first + part
            for f, v in enumerate((smooth, first, second)):
                filtered[f].append(v)
        mid_01[pl.ds(z0 + SUBS, LANES), :] = jnp.concatenate(filtered[0] + filtered[1], axis=0).T
        mid_02[pl.ds(z0 + SUBS, LANES), :] = jnp.concatenate(filtered[0] + filtered[2], axis=0).T
        return 0

    for c in range(chunks):
        for copy in fetches(c, after, before):
            copy.wait()
        lax.fori_loop(c * per, (c + 1) * per, along_y, 0, unroll=2)
    for buf in (mid_01, mid_02):
        buf[pl.ds(0, SUBS), :] = buf[pl.ds(depth, SUBS), :]
        buf[pl.ds(depth + SUBS, SUBS), :] = buf[pl.ds(SUBS, SUBS), :]

    n = 8
    lower = lax.broadcasted_iota(jnp.int32, (SUBS, LANES), 1) < LANES // 2
    mixed = [jnp.where(lower, along[2][HALO + k], along[0][HALO + k]) for k in range(HALO + 1)]

    def along_z(block, _):
        base = pl.multiple_of(block * (n * SUBS), n * SUBS)
        for j in range(n):
            at = base + SUBS * j + SUBS
            smooth = mid_01[pl.ds(at, SUBS), :] * along[0][HALO]
            first = None
            both = mid_02[pl.ds(at, SUBS), :] * mixed[0]
            for k in range(1, HALO + 1):
                up, down = mid_01[pl.ds(at + k, SUBS), :], mid_01[pl.ds(at - k, SUBS), :]
                smooth = smooth + (up + down) * along[0][HALO + k]
                part = (up - down) * along[1][HALO + k]
                first = part if first is None else first + part
                up, down = mid_02[pl.ds(at + k, SUBS), :], mid_02[pl.ds(at - k, SUBS), :]
                both = both + (up + down) * mixed[k]
            for i, v in enumerate((smooth, first, both)):
                field[pl.ds((base + SUBS * j) * CELL + i, SUBS, stride=CELL), :] = v
        return 0

    lax.fori_loop(0, depth // (n * SUBS), along_z, 0)
    field[pl.ds(depth * CELL, SUBS), :] = field[pl.ds(0, SUBS), :]


def woven(many, few):
    each = max(len(many) // max(len(few), 1), 1)
    few = list(few)
    for i, step in enumerate(many):
        if i % each == 0 and few:
            few.pop(0)()
        step()
    for step in few:
        step()


def lookup_kernel(place, asked, field, out, found, at_v, plane_of, row_of, bin_of, at_s, sent, *, bands, planes, rows):
    me = place[0]
    homes = asked.shape[0] // bands
    first = jnp.maximum(me - 1, 0) * homes
    last = jnp.minimum(me + 2, bands) * homes
    along = taps()
    scale = np.float32((HALO / 3.0) ** 2)
    subs = lax.broadcasted_iota(jnp.int32, (SUBS, LANES), 0)

    def read_rows(i, _):
        for u in range(UNROLL):
            row = first + UNROLL * i + u
            cell, z, b = asked[row, 0:1, :], asked[row, 1:2, :], asked[row, 2:3, :]
            at_v[pl.ds(row, 1), :] = z * CELL
            plane_of[pl.ds(row, 1), :] = jnp.where(cell >= 0, (row // homes - me) * planes + cell // rows, -planes)
            row_of[pl.ds(row, 1), :] = cell % rows
            bin_of[pl.ds(row, 1), :] = b
        return 0

    lax.fori_loop(0, (last - first) // UNROLL, read_rows, 0)
    move = pltpu.make_async_copy(at_v, at_s, sent)
    move.start()

    def no_row(row, _):
        out[row] = jnp.zeros((6, LANES), jnp.float32)
        return 0

    lax.fori_loop(0, first, no_row, 0)
    lax.fori_loop(last, bands * homes, no_row, 0)
    move.wait()

    def gather(row, slot):
        def one_group(i):
            for j in range(i * SUBS, (i + 1) * SUBS):
                found[slot, pl.ds(j * SUBS, SUBS), :] = field[pl.ds(at_s[row, j], SUBS), :]

        return [functools.partial(one_group, i) for i in range(LANES // SUBS)]

    def finish(row, slot):
        picked = {}

        def turn(beyond, c):
            at = beyond * CELL + c
            groups = [found[slot, pl.ds(i * SUBS * SUBS + at, SUBS, stride=SUBS), :] for i in range(LANES // SUBS)]
            flipped = jnp.concatenate(groups, axis=0).T
            mine = jnp.broadcast_to(row_of[pl.ds(row, 1), :], (SUBS, LANES))
            for h, a in enumerate(HELD[c]):
                tiles = [flipped[(h * rows + r) * SUBS : (h * rows + r + 1) * SUBS] for r in range(rows)]
                pick = tiles[0]
                for r in range(1, rows):
                    pick = jnp.where(mine == r, tiles[r], pick)
                picked[beyond, a] = pick

        def total():
            away = subs - plane_of[pl.ds(row, 1), :]
            weights = [jnp.zeros((SUBS, LANES), jnp.float32)] * 3
            for k in range(-HALO, HALO + 1):
                here = away == k
                weights = [jnp.where(here, along[f][k + HALO] * scale, w) for f, w in enumerate(weights)]
            w = (bin_of[pl.ds(row, 1), :].astype(jnp.float32) + 0.5) * (1.0 / BINS)
            for a in range(6):
                value = (1.0 - w) * picked[0, a] + w * picked[1, a]
                out[row, a, :] = jnp.sum(value * weights[ALONG_X[a]], axis=0)

        return [functools.partial(turn, beyond, c) for c in range(CELL) for beyond in range(2)] + [total]

    woven(gather(first, 0), [])

    def some_rows(i, _):
        for u in range(UNROLL):
            row = first + UNROLL * i + u
            woven(gather(jnp.minimum(row + 1, last - 1), (u + 1) % 2), finish(row, u % 2))
        return 0

    lax.fori_loop(0, (last - first) // UNROLL, some_rows, 0)


def in_hbm(x):
    return pltpu.with_memory_space_constraint(x, pltpu.HBM)


def in_vmem(x):
    return pltpu.with_memory_space_constraint(x, pltpu.VMEM)


def body(potential, gal_cells, gal_z, gal_bins, gal_counts):
    bands = lax.axis_size("gx")
    homes = lax.axis_size("yz")
    planes, rows, depth = potential.shape
    tiles, slots = gal_cells.shape[2:]
    assert planes == SUBS and rows == SUBS and slots == LANES and homes % UNROLL == 0
    vmem = pl.BlockSpec(memory_space=pltpu.VMEM)
    smem = pl.BlockSpec(memory_space=pltpu.SMEM)

    parity = (lax.axis_index("yz") % 2).reshape(1)
    hbm = pl.BlockSpec(memory_space=pltpu.HBM)
    field_shape = (depth * CELL + SUBS, LANES)
    halo_shape = (HALO, planes, depth)
    pair_out, next_out, asked, hold = pl.pallas_call(
        functools.partial(send_kernel, bands=bands, rows=rows),
        out_shape=(
            jax.ShapeDtypeStruct(halo_shape, jnp.float32),
            jax.ShapeDtypeStruct(halo_shape, jnp.float32),
            jax.ShapeDtypeStruct((bands * tiles, 3, slots), jnp.int32),
            pltpu.VMEM(field_shape, jnp.float32),
        ),
        in_specs=[smem] + [hbm] * 5,
        out_specs=(hbm, hbm, hbm, vmem),
        scratch_shapes=[
            pltpu.SMEM((1, tiles), jnp.int32),
            pltpu.VMEM((tiles, slots), jnp.int32),
            pltpu.VMEM((tiles, slots), jnp.int32),
            pltpu.VMEM((tiles, slots), jnp.int32),
            pltpu.VMEM(potential.shape, jnp.float32),
            pltpu.VMEM((bands * tiles, 3, slots), jnp.int32),
            pltpu.SemaphoreType.DMA((planes + 4,)),
            pltpu.SemaphoreType.DMA((3, HALO)),
        ],
        compiler_params=pltpu.CompilerParams(vmem_limit_bytes=8 << 20),
    )(
        parity,
        in_hbm(gal_counts.reshape(1, tiles)),
        in_hbm(gal_cells.reshape(tiles, slots)),
        in_hbm(gal_z.reshape(tiles, slots)),
        in_hbm(gal_bins.reshape(tiles, slots)),
        in_hbm(potential),
    )

    swap = lambda first: [p for i in range(first, homes - 1, 2) for p in ((i, i + 1), (i + 1, i))]
    pair_in = lax.ppermute(pair_out, "yz", swap(0))
    next_in = lax.ppermute(next_out, "yz", swap(1))
    asked = lax.all_to_all(asked, ("gx", "yz"), split_axis=0, concat_axis=0, tiled=True)

    chunks = 4
    mid_shape = (depth + 2 * SUBS, LANES)
    field = pl.pallas_call(
        functools.partial(field_kernel, rows=rows, depth=depth, chunks=chunks),
        out_shape=pltpu.VMEM(field_shape, jnp.float32),
        in_specs=[smem, hbm, hbm, hbm, vmem],
        out_specs=vmem,
        input_output_aliases={4: 0},
        scratch_shapes=[
            pltpu.VMEM(halo_shape, jnp.float32),
            pltpu.VMEM(halo_shape, jnp.float32),
            pltpu.VMEM((rows, planes, depth), jnp.float32),
            pltpu.VMEM(mid_shape, jnp.float32),
            pltpu.VMEM(mid_shape, jnp.float32),
            pltpu.SemaphoreType.DMA((chunks, 2 + planes)),
        ],
        compiler_params=pltpu.CompilerParams(vmem_limit_bytes=24 << 20),
    )(parity, in_hbm(pair_in), in_hbm(potential), in_hbm(next_in), in_vmem(hold))

    me = lax.axis_index("gx")
    queries = (bands * homes, slots)
    served = pl.pallas_call(
        functools.partial(lookup_kernel, bands=bands, planes=planes, rows=rows),
        out_shape=jax.ShapeDtypeStruct((bands * homes, 6, slots), jnp.float32),
        in_specs=[smem, vmem, vmem],
        out_specs=vmem,
        scratch_shapes=[pltpu.VMEM((2, LANES * SUBS + SUBS, LANES), jnp.float32)]
        + [pltpu.VMEM(queries, jnp.int32)] * 4
        + [pltpu.SMEM(queries, jnp.int32), pltpu.SemaphoreType.DMA],
        compiler_params=pltpu.CompilerParams(vmem_limit_bytes=24 << 20),
    )(me.reshape(1), asked, in_vmem(field))

    returned = lax.all_to_all(served, ("gx", "yz"), split_axis=0, concat_axis=0, tiled=True)
    total = jnp.sum(returned.reshape(bands, tiles, 6, slots), axis=0)
    return total.transpose(1, 0, 2).reshape(6, 1, 1, tiles * slots)


def solution(mesh):
    return jax.shard_map(
        body,
        mesh=mesh,
        in_specs=(
            P("gx", "yz", None),
            P("gx", "yz", None, None),
            P("gx", "yz", None, None),
            P("gx", "yz", None, None),
            P("gx", "yz", None),
        ),
        out_specs=P(None, "gx", "yz", None),
        check_vma=False,
    )
```

```python
import functools

import jax
import jax.numpy as jnp
import numpy as np
from jax import lax
from jax.experimental import pallas as pl
from jax.experimental.pallas import tpu as pltpu
from jax.sharding import PartitionSpec as P


HALO = 6
BINS = 8
LANES = 128
SUBS = 8
UNROLL = 4
CELL = 3
HELD = ((0, 3), (4, 5), (2, 1))
ALONG_X = (2, 0, 0, 1, 1, 0)


def taps():
    offsets = np.arange(-HALO, HALO + 1).astype(np.float32)
    sigma = np.float32(HALO / 3.0)
    smooth = np.exp(-offsets * offsets / (2 * sigma * sigma)).astype(np.float32)
    smooth = smooth / np.sum(smooth, dtype=np.float32)
    first = offsets / (sigma * sigma) * smooth
    second = (offsets * offsets / sigma**4 - 1 / (sigma * sigma)) * smooth
    return np.stack([smooth, first, second]).astype(np.float32)


def send_kernel(
    parity, counts_in, cells_in, zeds_in, bins_in, own_in, pair_out, next_out, asked_out, hold,
    counts, cells, zeds, bins, own, asked, came, gone, *, bands, rows
):
    fetches = [pltpu.make_async_copy(own_in.at[x], own.at[x], came.at[x]) for x in range(own.shape[0])]
    small = ((counts_in, counts), (cells_in, cells), (zeds_in, zeds), (bins_in, bins))
    small = [pltpu.make_async_copy(a, b, came.at[own.shape[0] + i]) for i, (a, b) in enumerate(small)]
    for copy in small + fetches:
        copy.start()
    for copy in small:
        copy.wait()
    tiles, slots = cells.shape
    slot = lax.broadcasted_iota(jnp.int32, (1, slots), 1)
    for t in range(tiles):
        cell = jnp.where(slot < counts[0, t], cells[t : t + 1, :], -1)
        query = jnp.concatenate([cell, zeds[t : t + 1, :] * CELL, bins[t : t + 1, :]], axis=0)
        for band in range(bands):
            asked[band * tiles + t] = query
    moves = [pltpu.make_async_copy(asked, asked_out, gone.at[2, 0])]
    moves[0].start()
    for copy in fetches:
        copy.wait()
    to_pair = (rows - HALO) * (1 - parity[0])
    to_next = (rows - HALO) * parity[0]
    for y in range(HALO):
        moves.append(pltpu.make_async_copy(own.at[:, to_pair + y, :], pair_out.at[y], gone.at[0, y]))
        moves.append(pltpu.make_async_copy(own.at[:, to_next + y, :], next_out.at[y], gone.at[1, y]))
    for copy in moves[1:]:
        copy.start()
    for copy in moves:
        copy.wait()


def field_kernel(parity, pair_in, next_in, pair_out, next_out, hold, field, before, after, own, mid_01, mid_02, came, *, rows, depth, chunks):
    along = taps()
    size = depth // chunks
    per = size // LANES

    kept = rows - HALO

    def fetches(c, is_even):
        zs = pl.ds(c * size, size)
        low, high = (next_out, pair_out) if is_even else (pair_out, next_out)
        above, below = (pair_in, next_in) if is_even else (next_in, pair_in)
        moves = (
            (below.at[:, :, zs], before.at[:, :, zs]),
            (low.at[pl.ds(0, kept), :, zs], own.at[pl.ds(0, kept), :, zs]),
            (high.at[:, :, zs], own.at[pl.ds(kept, HALO), :, zs]),
            (above.at[:, :, zs], after.at[:, :, zs]),
        )
        return [pltpu.make_async_copy(*move, came.at[c, i]) for i, move in enumerate(moves)]

    even = parity[0] == 0
    for is_even in (True, False):

        @pl.when(even if is_even else jnp.logical_not(even))
        def _():
            for c in range(chunks):
                for copy in fetches(c, is_even):
                    copy.start()

    def along_y(block, _):
        z0 = pl.multiple_of(block * LANES, LANES)
        zs = pl.ds(z0, LANES)
        u = [before[y, :, zs] for y in range(HALO)]
        u += [own[y, :, zs] for y in range(rows)]
        u += [after[y, :, zs] for y in range(HALO)]
        filtered = [[], [], []]
        for r in range(rows):
            c = u[r + HALO]
            smooth = c * along[0][HALO]
            second = c * along[2][HALO]
            first = None
            for k in range(1, HALO + 1):
                up, down = u[r + HALO + k], u[r + HALO - k]
                both = up + down
                smooth = smooth + both * along[0][HALO + k]
                second = second + both * along[2][HALO + k]
                part = (up - down) * along[1][HALO + k]
                first = part if first is None else first + part
            for f, v in enumerate((smooth, first, second)):
                filtered[f].append(v)
        mid_01[pl.ds(z0 + SUBS, LANES), :] = jnp.concatenate(filtered[0] + filtered[1], axis=0).T
        mid_02[pl.ds(z0 + SUBS, LANES), :] = jnp.concatenate(filtered[0] + filtered[2], axis=0).T
        return 0

    for c in range(chunks):
        for copy in fetches(c, True):
            copy.wait()
        lax.fori_loop(c * per, (c + 1) * per, along_y, 0, unroll=4)
    for buf in (mid_01, mid_02):
        buf[pl.ds(0, SUBS), :] = buf[pl.ds(depth, SUBS), :]
        buf[pl.ds(depth + SUBS, SUBS), :] = buf[pl.ds(SUBS, SUBS), :]

    n = 8
    lower = lax.broadcasted_iota(jnp.int32, (SUBS, LANES), 1) < LANES // 2
    mixed = [jnp.where(lower, along[2][HALO + k], along[0][HALO + k]) for k in range(HALO + 1)]

    def along_z(block, _):
        base = pl.multiple_of(block * (n * SUBS), n * SUBS)
        for j in range(n):
            at = base + SUBS * j + SUBS
            smooth = mid_01[pl.ds(at, SUBS), :] * along[0][HALO]
            first = None
            both = mid_02[pl.ds(at, SUBS), :] * mixed[0]
            for k in range(1, HALO + 1):
                up, down = mid_01[pl.ds(at + k, SUBS), :], mid_01[pl.ds(at - k, SUBS), :]
                smooth = smooth + (up + down) * along[0][HALO + k]
                part = (up - down) * along[1][HALO + k]
                first = part if first is None else first + part
                up, down = mid_02[pl.ds(at + k, SUBS), :], mid_02[pl.ds(at - k, SUBS), :]
                both = both + (up + down) * mixed[k]
            for i, v in enumerate((smooth, first, both)):
                field[pl.ds((base + SUBS * j) * CELL + i, SUBS, stride=CELL), :] = v
        return 0

    lax.fori_loop(0, depth // (n * SUBS), along_z, 0)
    field[pl.ds(depth * CELL, SUBS), :] = field[pl.ds(0, SUBS), :]


def woven(many, few):
    each = max(len(many) // max(len(few), 1), 1)
    few = list(few)
    for i, step in enumerate(many):
        if i % each == 0 and few:
            few.pop(0)()
        step()
    for step in few:
        step()


def lookup_kernel(place, asked, field, out, found, plane_of, row_of, bin_of, at_s, sent, *, bands, planes, rows):
    me = place[0]
    homes = asked.shape[0] // bands
    first = jnp.maximum(me - 1, 0) * homes
    last = jnp.minimum(me + 2, bands) * homes
    along = taps()
    scale = np.float32((HALO / 3.0) ** 2)
    subs = lax.broadcasted_iota(jnp.int32, (SUBS, LANES), 0)

    move = pltpu.make_async_copy(asked.at[:, 1, :], at_s, sent)
    move.start()

    def read_rows(i, _):
        for u in range(UNROLL):
            row = first + UNROLL * i + u
            cell, b = asked[row, 0:1, :], asked[row, 2:3, :]
            plane_of[pl.ds(row, 1), :] = jnp.where(cell >= 0, (row // homes - me) * planes + cell // rows, -planes)
            row_of[pl.ds(row, 1), :] = cell % rows
            bin_of[pl.ds(row, 1), :] = b
        return 0

    lax.fori_loop(0, (last - first) // UNROLL, read_rows, 0)

    def no_row(row, _):
        out[row] = jnp.zeros((6, LANES), jnp.float32)
        return 0

    lax.fori_loop(0, first, no_row, 0)
    lax.fori_loop(last, bands * homes, no_row, 0)
    move.wait()

    def gather(row, slot):
        def one_group(i):
            for j in range(i * SUBS, (i + 1) * SUBS):
                found[slot, pl.ds(j * SUBS, SUBS), :] = field[pl.ds(at_s[row, j], SUBS), :]

        return [functools.partial(one_group, i) for i in range(LANES // SUBS)]

    def finish(row, slot):
        picked = {}

        def turn(beyond, c):
            at = beyond * CELL + c
            groups = [found[slot, pl.ds(i * SUBS * SUBS + at, SUBS, stride=SUBS), :] for i in range(LANES // SUBS)]
            flipped = jnp.concatenate(groups, axis=0).T
            mine = jnp.broadcast_to(row_of[pl.ds(row, 1), :], (SUBS, LANES))
            for h, a in enumerate(HELD[c]):
                tiles = [flipped[(h * rows + r) * SUBS : (h * rows + r + 1) * SUBS] for r in range(rows)]
                pick = tiles[0]
                for r in range(1, rows):
                    pick = jnp.where(mine == r, tiles[r], pick)
                picked[beyond, a] = pick

        def total():
            away = subs - plane_of[pl.ds(row, 1), :]
            weights = [jnp.zeros((SUBS, LANES), jnp.float32)] * 3
            for k in range(-HALO, HALO + 1):
                here = away == k
                weights = [jnp.where(here, along[f][k + HALO] * scale, w) for f, w in enumerate(weights)]
            w = (bin_of[pl.ds(row, 1), :].astype(jnp.float32) + 0.5) * (1.0 / BINS)
            for a in range(6):
                value = (1.0 - w) * picked[0, a] + w * picked[1, a]
                out[row, a, :] = jnp.sum(value * weights[ALONG_X[a]], axis=0)

        return [functools.partial(turn, beyond, c) for c in range(CELL) for beyond in range(2)] + [total]

    woven(gather(first, 0), [])

    def some_rows(i, _):
        for u in range(UNROLL):
            row = first + UNROLL * i + u
            woven(gather(jnp.minimum(row + 1, last - 1), (u + 1) % 2), finish(row, u % 2))
        return 0

    lax.fori_loop(0, (last - first) // UNROLL, some_rows, 0)


def in_hbm(x):
    return pltpu.with_memory_space_constraint(x, pltpu.HBM)


def in_vmem(x):
    return pltpu.with_memory_space_constraint(x, pltpu.VMEM)


def body(potential, gal_cells, gal_z, gal_bins, gal_counts):
    bands = lax.axis_size("gx")
    homes = lax.axis_size("yz")
    planes, rows, depth = potential.shape
    tiles, slots = gal_cells.shape[2:]
    assert planes == SUBS and rows == SUBS and slots == LANES and homes % UNROLL == 0
    vmem = pl.BlockSpec(memory_space=pltpu.VMEM)
    smem = pl.BlockSpec(memory_space=pltpu.SMEM)

    parity = (lax.axis_index("yz") % 2).reshape(1)
    hbm = pl.BlockSpec(memory_space=pltpu.HBM)
    field_shape = (depth * CELL + SUBS, LANES)
    halo_shape = (HALO, planes, depth)
    pair_out, next_out, asked, hold = pl.pallas_call(
        functools.partial(send_kernel, bands=bands, rows=rows),
        out_shape=(
            pltpu.HBM(halo_shape, jnp.float32),
            pltpu.HBM(halo_shape, jnp.float32),
            pltpu.HBM((bands * tiles, 3, slots), jnp.int32),
            pltpu.VMEM(field_shape, jnp.float32),
        ),
        in_specs=[smem] + [hbm] * 5,
        out_specs=(hbm, hbm, hbm, vmem),
        scratch_shapes=[
            pltpu.SMEM((1, tiles), jnp.int32),
            pltpu.VMEM((tiles, slots), jnp.int32),
            pltpu.VMEM((tiles, slots), jnp.int32),
            pltpu.VMEM((tiles, slots), jnp.int32),
            pltpu.VMEM(potential.shape, jnp.float32),
            pltpu.VMEM((bands * tiles, 3, slots), jnp.int32),
            pltpu.SemaphoreType.DMA((planes + 4,)),
            pltpu.SemaphoreType.DMA((3, HALO)),
        ],
        compiler_params=pltpu.CompilerParams(vmem_limit_bytes=8 << 20),
    )(
        parity,
        in_hbm(gal_counts.reshape(1, tiles)),
        in_hbm(gal_cells.reshape(tiles, slots)),
        in_hbm(gal_z.reshape(tiles, slots)),
        in_hbm(gal_bins.reshape(tiles, slots)),
        in_hbm(potential),
    )

    swap = lambda first: [p for i in range(first, homes - 1, 2) for p in ((i, i + 1), (i + 1, i))]
    pair_in = lax.ppermute(pair_out, "yz", swap(0))
    next_in = lax.ppermute(next_out, "yz", swap(1))
    asked = lax.all_to_all(asked, ("gx", "yz"), split_axis=0, concat_axis=0, tiled=True)

    chunks = 2
    mid_shape = (depth + 2 * SUBS, LANES)
    field = pl.pallas_call(
        functools.partial(field_kernel, rows=rows, depth=depth, chunks=chunks),
        out_shape=pltpu.VMEM(field_shape, jnp.float32),
        in_specs=[smem, hbm, hbm, hbm, hbm, vmem],
        out_specs=vmem,
        input_output_aliases={5: 0},
        scratch_shapes=[
            pltpu.VMEM(halo_shape, jnp.float32),
            pltpu.VMEM(halo_shape, jnp.float32),
            pltpu.VMEM((rows, planes, depth), jnp.float32),
            pltpu.VMEM(mid_shape, jnp.float32),
            pltpu.VMEM(mid_shape, jnp.float32),
            pltpu.SemaphoreType.DMA((chunks, 4)),
        ],
        compiler_params=pltpu.CompilerParams(vmem_limit_bytes=24 << 20),
    )(parity, in_hbm(pair_in), in_hbm(next_in), in_hbm(pair_out), in_hbm(next_out), in_vmem(hold))

    me = lax.axis_index("gx")
    queries = (bands * homes, slots)
    served = pl.pallas_call(
        functools.partial(lookup_kernel, bands=bands, planes=planes, rows=rows),
        out_shape=jax.ShapeDtypeStruct((bands * homes, 6, slots), jnp.float32),
        in_specs=[smem, vmem, vmem],
        out_specs=vmem,
        scratch_shapes=[pltpu.VMEM((2, LANES * SUBS + SUBS, LANES), jnp.float32)]
        + [pltpu.VMEM(queries, jnp.int32)] * 3
        + [pltpu.SMEM(queries, jnp.int32), pltpu.SemaphoreType.DMA],
        compiler_params=pltpu.CompilerParams(vmem_limit_bytes=24 << 20),
    )(me.reshape(1), in_vmem(asked), in_vmem(field))

    returned = lax.all_to_all(served, ("gx", "yz"), split_axis=0, concat_axis=0, tiled=True)
    total = jnp.sum(returned.reshape(bands, tiles, 6, slots), axis=0)
    return total.transpose(1, 0, 2).reshape(6, 1, 1, tiles * slots)


def solution(mesh):
    return jax.shard_map(
        body,
        mesh=mesh,
        in_specs=(
            P("gx", "yz", None),
            P("gx", "yz", None, None),
            P("gx", "yz", None, None),
            P("gx", "yz", None, None),
            P("gx", "yz", None),
        ),
        out_specs=P(None, "gx", "yz", None),
        check_vma=False,
    )
```

```python
import functools

import jax
import jax.numpy as jnp
import numpy as np
from jax import lax
from jax.experimental import pallas as pl
from jax.experimental.pallas import tpu as pltpu
from jax.sharding import PartitionSpec as P


HALO = 6
BINS = 8
LANES = 128
SUBS = 8
EDGES = (1, 4)
STEPS = 4
UNROLL = 4
CELL = 3
HELD = ((0, 3), (4, 5), (2, 1))
ALONG_X = (2, 0, 0, 1, 1, 0)


def taps():
    offsets = np.arange(-HALO, HALO + 1).astype(np.float32)
    sigma = np.float32(HALO / 3.0)
    smooth = np.exp(-offsets * offsets / (2 * sigma * sigma)).astype(np.float32)
    smooth = smooth / np.sum(smooth, dtype=np.float32)
    first = offsets / (sigma * sigma) * smooth
    second = (offsets * offsets / sigma**4 - 1 / (sigma * sigma)) * smooth
    return np.stack([smooth, first, second]).astype(np.float32)


def send_kernel(
    parity, counts_in, cells_in, zeds_in, bins_in, own_in, pair_out, next_out, asked_out, hold,
    counts, cells, zeds, bins, own, asked, came, gone, *, bands, rows
):
    fetches = [pltpu.make_async_copy(own_in.at[x], own.at[x], came.at[x]) for x in range(own.shape[0])]
    small = ((counts_in, counts), (cells_in, cells), (zeds_in, zeds), (bins_in, bins))
    small = [pltpu.make_async_copy(a, b, came.at[own.shape[0] + i]) for i, (a, b) in enumerate(small)]
    for copy in small + fetches:
        copy.start()
    for copy in small:
        copy.wait()
    tiles, slots = cells.shape
    slot = lax.broadcasted_iota(jnp.int32, (1, slots), 1)
    for t in range(tiles):
        cell = jnp.where(slot < counts[0, t], cells[t : t + 1, :], -1)
        query = jnp.concatenate([cell, zeds[t : t + 1, :] * CELL, bins[t : t + 1, :]], axis=0)
        for band in range(bands):
            asked[band * tiles + t] = query
    moves = [pltpu.make_async_copy(asked, asked_out, gone.at[2, 0])]
    moves[0].start()
    for copy in fetches:
        copy.wait()
    to_pair = (rows - HALO) * (1 - parity[0])
    to_next = (rows - HALO) * parity[0]
    for y in range(HALO):
        moves.append(pltpu.make_async_copy(own.at[:, to_pair + y, :], pair_out.at[y], gone.at[0, y]))
        moves.append(pltpu.make_async_copy(own.at[:, to_next + y, :], next_out.at[y], gone.at[1, y]))
    for copy in moves[1:]:
        copy.start()
    for copy in moves:
        copy.wait()


def field_kernel(parity, pair_in, next_in, pair_out, next_out, hold, field, before, after, own, mid_01, mid_02, came, *, rows, depth, chunks):
    along = taps()
    per = depth // LANES // STEPS
    edges = [0] + [per * e for e in EDGES]

    kept = rows - HALO

    def fetches(c, is_even):
        zs = pl.ds(edges[c] * LANES, (edges[c + 1] - edges[c]) * LANES)
        low, high = (next_out, pair_out) if is_even else (pair_out, next_out)
        above, below = (pair_in, next_in) if is_even else (next_in, pair_in)
        moves = (
            (below.at[:, :, zs], before.at[:, :, zs]),
            (low.at[pl.ds(0, kept), :, zs], own.at[pl.ds(0, kept), :, zs]),
            (high.at[:, :, zs], own.at[pl.ds(kept, HALO), :, zs]),
            (above.at[:, :, zs], after.at[:, :, zs]),
        )
        return [pltpu.make_async_copy(*move, came.at[c, i]) for i, move in enumerate(moves)]

    even = parity[0] == 0
    for is_even in (True, False):

        @pl.when(even if is_even else jnp.logical_not(even))
        def _():
            for c in range(chunks):
                for copy in fetches(c, is_even):
                    copy.start()

    def along_y(block, _):
        z0 = pl.multiple_of(block * LANES, LANES)
        zs = pl.ds(z0, LANES)
        u = [before[y, :, zs] for y in range(HALO)]
        u += [own[y, :, zs] for y in range(rows)]
        u += [after[y, :, zs] for y in range(HALO)]
        filtered = [[], [], []]
        for r in range(rows):
            c = u[r + HALO]
            smooth = c * along[0][HALO]
            second = c * along[2][HALO]
            first = None
            for k in range(1, HALO + 1):
                up, down = u[r + HALO + k], u[r + HALO - k]
                both = up + down
                smooth = smooth + both * along[0][HALO + k]
                second = second + both * along[2][HALO + k]
                part = (up - down) * along[1][HALO + k]
                first = part if first is None else first + part
            for f, v in enumerate((smooth, first, second)):
                filtered[f].append(v)
        mid_01[pl.ds(z0 + SUBS, LANES), :] = jnp.concatenate(filtered[0] + filtered[1], axis=0).T
        mid_02[pl.ds(z0 + SUBS, LANES), :] = jnp.concatenate(filtered[0] + filtered[2], axis=0).T
        return 0

    for c in range(chunks):
        for copy in fetches(c, True):
            copy.wait()
        lax.fori_loop(edges[c], edges[c + 1], along_y, 0, unroll=4)
    for buf in (mid_01, mid_02):
        buf[pl.ds(0, SUBS), :] = buf[pl.ds(depth, SUBS), :]
        buf[pl.ds(depth + SUBS, SUBS), :] = buf[pl.ds(SUBS, SUBS), :]

    n = 32
    lower = lax.broadcasted_iota(jnp.int32, (SUBS, LANES), 1) < LANES // 2
    mixed = [jnp.where(lower, along[2][HALO + k], along[0][HALO + k]) for k in range(HALO + 1)]

    def along_z(block, _):
        base = pl.multiple_of(block * (n * SUBS), n * SUBS)
        for j in range(n):
            at = base + SUBS * j + SUBS
            smooth = mid_01[pl.ds(at, SUBS), :] * along[0][HALO]
            first = None
            both = mid_02[pl.ds(at, SUBS), :] * mixed[0]
            for k in range(1, HALO + 1):
                up, down = mid_01[pl.ds(at + k, SUBS), :], mid_01[pl.ds(at - k, SUBS), :]
                smooth = smooth + (up + down) * along[0][HALO + k]
                part = (up - down) * along[1][HALO + k]
                first = part if first is None else first + part
                up, down = mid_02[pl.ds(at + k, SUBS), :], mid_02[pl.ds(at - k, SUBS), :]
                both = both + (up + down) * mixed[k]
            for i, v in enumerate((smooth, first, both)):
                field[pl.ds((base + SUBS * j) * CELL + i, SUBS, stride=CELL), :] = v
        return 0

    lax.fori_loop(0, depth // (n * SUBS), along_z, 0)
    field[pl.ds(depth * CELL, SUBS), :] = field[pl.ds(0, SUBS), :]


def woven(many, few):
    each = max(len(many) // max(len(few), 1), 1)
    few = list(few)
    for i, step in enumerate(many):
        if i % each == 0 and few:
            few.pop(0)()
        step()
    for step in few:
        step()


def lookup_kernel(place, asked, field, out, found, plane_of, row_of, bin_of, at_s, sent, *, bands, planes, rows):
    me = place[0]
    homes = asked.shape[0] // bands
    first = jnp.maximum(me - 1, 0) * homes
    last = jnp.minimum(me + 2, bands) * homes
    along = taps()
    scale = np.float32((HALO / 3.0) ** 2)
    subs = lax.broadcasted_iota(jnp.int32, (SUBS, LANES), 0)

    move = pltpu.make_async_copy(asked.at[:, 1, :], at_s, sent)
    move.start()

    def read_rows(i, _):
        for u in range(UNROLL):
            row = first + UNROLL * i + u
            cell, b = asked[row, 0:1, :], asked[row, 2:3, :]
            plane_of[pl.ds(row, 1), :] = jnp.where(cell >= 0, (row // homes - me) * planes + cell // rows, -planes)
            row_of[pl.ds(row, 1), :] = cell % rows
            bin_of[pl.ds(row, 1), :] = b
        return 0

    lax.fori_loop(0, (last - first) // UNROLL, read_rows, 0)

    def no_row(row, _):
        out[row] = jnp.zeros((1, 6 * LANES), jnp.float32)
        return 0

    lax.fori_loop(0, first, no_row, 0)
    lax.fori_loop(last, bands * homes, no_row, 0)
    move.wait()

    def gather(row, slot):
        def one_group(i):
            for j in range(i * SUBS, (i + 1) * SUBS):
                found[slot, pl.ds(j * SUBS, SUBS), :] = field[pl.ds(at_s[row, j], SUBS), :]

        return [functools.partial(one_group, i) for i in range(LANES // SUBS)]

    def finish(row, slot):
        picked = {}

        def turn(beyond, c):
            at = beyond * CELL + c
            groups = [found[slot, pl.ds(i * SUBS * SUBS + at, SUBS, stride=SUBS), :] for i in range(LANES // SUBS)]
            flipped = jnp.concatenate(groups, axis=0).T
            mine = jnp.broadcast_to(row_of[pl.ds(row, 1), :], (SUBS, LANES))
            for h, a in enumerate(HELD[c]):
                tiles = [flipped[(h * rows + r) * SUBS : (h * rows + r + 1) * SUBS] for r in range(rows)]
                pick = tiles[0]
                for r in range(1, rows):
                    pick = jnp.where(mine == r, tiles[r], pick)
                picked[beyond, a] = pick

        def total():
            away = subs - plane_of[pl.ds(row, 1), :]
            weights = [jnp.zeros((SUBS, LANES), jnp.float32)] * 3
            for k in range(-HALO, HALO + 1):
                here = away == k
                weights = [jnp.where(here, along[f][k + HALO] * scale, w) for f, w in enumerate(weights)]
            w = (bin_of[pl.ds(row, 1), :].astype(jnp.float32) + 0.5) * (1.0 / BINS)
            for a in range(6):
                value = (1.0 - w) * picked[0, a] + w * picked[1, a]
                out[row, :, pl.ds(a * LANES, LANES)] = jnp.sum(value * weights[ALONG_X[a]], axis=0, keepdims=True)

        return [functools.partial(turn, beyond, c) for c in range(CELL) for beyond in range(2)] + [total]

    woven(gather(first, 0), [])

    def some_rows(i, _):
        for u in range(UNROLL):
            row = first + UNROLL * i + u
            woven(gather(jnp.minimum(row + 1, last - 1), (u + 1) % 2), finish(row, u % 2))
        return 0

    lax.fori_loop(0, (last - first) // UNROLL, some_rows, 0)


def in_hbm(x):
    return pltpu.with_memory_space_constraint(x, pltpu.HBM)


def in_vmem(x):
    return pltpu.with_memory_space_constraint(x, pltpu.VMEM)


def body(potential, gal_cells, gal_z, gal_bins, gal_counts):
    bands = lax.axis_size("gx")
    homes = lax.axis_size("yz")
    planes, rows, depth = potential.shape
    tiles, slots = gal_cells.shape[2:]
    assert planes == SUBS and rows == SUBS and slots == LANES and homes % UNROLL == 0
    vmem = pl.BlockSpec(memory_space=pltpu.VMEM)
    smem = pl.BlockSpec(memory_space=pltpu.SMEM)

    parity = (lax.axis_index("yz") % 2).reshape(1)
    hbm = pl.BlockSpec(memory_space=pltpu.HBM)
    field_shape = (depth * CELL + SUBS, LANES)
    halo_shape = (HALO, planes, depth)
    pair_out, next_out, asked, hold = pl.pallas_call(
        functools.partial(send_kernel, bands=bands, rows=rows),
        out_shape=(
            pltpu.HBM(halo_shape, jnp.float32),
            pltpu.HBM(halo_shape, jnp.float32),
            pltpu.HBM((bands * tiles, 3, slots), jnp.int32),
            pltpu.VMEM(field_shape, jnp.float32),
        ),
        in_specs=[smem] + [hbm] * 5,
        out_specs=(hbm, hbm, hbm, vmem),
        scratch_shapes=[
            pltpu.SMEM((1, tiles), jnp.int32),
            pltpu.VMEM((tiles, slots), jnp.int32),
            pltpu.VMEM((tiles, slots), jnp.int32),
            pltpu.VMEM((tiles, slots), jnp.int32),
            pltpu.VMEM(potential.shape, jnp.float32),
            pltpu.VMEM((bands * tiles, 3, slots), jnp.int32),
            pltpu.SemaphoreType.DMA((planes + 4,)),
            pltpu.SemaphoreType.DMA((3, HALO)),
        ],
        compiler_params=pltpu.CompilerParams(vmem_limit_bytes=8 << 20),
    )(
        parity,
        in_hbm(gal_counts.reshape(1, tiles)),
        in_hbm(gal_cells.reshape(tiles, slots)),
        in_hbm(gal_z.reshape(tiles, slots)),
        in_hbm(gal_bins.reshape(tiles, slots)),
        in_hbm(potential),
    )

    swap = lambda first: [p for i in range(first, homes - 1, 2) for p in ((i, i + 1), (i + 1, i))]
    pair_in = lax.ppermute(pair_out, "yz", swap(0))
    next_in = lax.ppermute(next_out, "yz", swap(1))
    asked = lax.all_to_all(asked, ("gx", "yz"), split_axis=0, concat_axis=0, tiled=True)

    chunks = len(EDGES)
    mid_shape = (depth + 2 * SUBS, LANES)
    field = pl.pallas_call(
        functools.partial(field_kernel, rows=rows, depth=depth, chunks=chunks),
        out_shape=pltpu.VMEM(field_shape, jnp.float32),
        in_specs=[smem, hbm, hbm, hbm, hbm, vmem],
        out_specs=vmem,
        input_output_aliases={5: 0},
        scratch_shapes=[
            pltpu.VMEM(halo_shape, jnp.float32),
            pltpu.VMEM(halo_shape, jnp.float32),
            pltpu.VMEM((rows, planes, depth), jnp.float32),
            pltpu.VMEM(mid_shape, jnp.float32),
            pltpu.VMEM(mid_shape, jnp.float32),
            pltpu.SemaphoreType.DMA((chunks, 4)),
        ],
        compiler_params=pltpu.CompilerParams(vmem_limit_bytes=24 << 20),
    )(parity, in_hbm(pair_in), in_hbm(next_in), in_hbm(pair_out), in_hbm(next_out), in_vmem(hold))

    me = lax.axis_index("gx")
    queries = (bands * homes, slots)
    served = pl.pallas_call(
        functools.partial(lookup_kernel, bands=bands, planes=planes, rows=rows),
        out_shape=jax.ShapeDtypeStruct((bands * homes, 1, 6 * slots), jnp.float32),
        in_specs=[smem, vmem, vmem],
        out_specs=vmem,
        scratch_shapes=[pltpu.VMEM((2, LANES * SUBS + SUBS, LANES), jnp.float32)]
        + [pltpu.VMEM(queries, jnp.int32)] * 3
        + [pltpu.SMEM(queries, jnp.int32), pltpu.SemaphoreType.DMA],
        compiler_params=pltpu.CompilerParams(vmem_limit_bytes=24 << 20),
    )(me.reshape(1), in_vmem(asked), in_vmem(field))

    returned = lax.all_to_all(served, ("gx", "yz"), split_axis=0, concat_axis=0, tiled=True)
    total = jnp.sum(returned.reshape(bands, tiles, 6, slots), axis=0)
    return total.transpose(1, 0, 2).reshape(6, 1, 1, tiles * slots)


def solution(mesh):
    return jax.shard_map(
        body,
        mesh=mesh,
        in_specs=(
            P("gx", "yz", None),
            P("gx", "yz", None, None),
            P("gx", "yz", None, None),
            P("gx", "yz", None, None),
            P("gx", "yz", None),
        ),
        out_specs=P(None, "gx", "yz", None),
        check_vma=False,
    )
```
